1024 devices in a mesh: seq: 128 (over z, x, core), tile: 8 (over y).
Axes of the slice: x: 8, y: 8, z: 8, core: 2. Of those that a mesh axis runs over, the one named last changes fastest.
Arguments:
- query_feat: float32 [24576, 4096], P('seq', 'tile'), may hold values from -6 to 6
- key_feat: float32 [24576, 4096], P('seq', 'tile'), may hold values from -6 to 6
- value_feat: float32 [24576, 4096], P('seq', 'tile'), may hold values from -6 to 6
- short_filter: float32 [3, 7, 4096], P(None, None, 'tile'), may hold values from -3 to 3
- medium_filter: float32 [128, 4096], P(None, 'tile'), may hold values from -0.6 to 0.6
- out_weight: bfloat16 [4096, 4096], P('tile'), may hold values from -0.09375 to 0.09375
- cotangent: bfloat16 [24576, 4096], P('seq', 'tile'), may hold values from -6 to 6
Outputs:
- block_out: float32 [24576, 4096], P('seq', 'tile')
- grad_query: float32 [24576, 4096], P('seq', 'tile')
- grad_key: float32 [24576, 4096], P('seq', 'tile')
- grad_value: float32 [24576, 4096], P('seq', 'tile')
- grad_short: float32 [3, 7, 4096], P(None, None, 'tile')
- grad_medium: float32 [128, 4096], P(None, 'tile')
The draws below stay inside these ranges and needn't reach their ends.
All inputs are finite; a program needn't handle non-finite values.
Results may differ from the reference program's by a relative error of at most 0.0029.
Values may be sent and summed in bfloat16 or wider, within the bound.
No kernel may reach another device: no remote copies, remote signals or barrier semaphores. Data moves between devices by JAX's collectives and lax.ppermute only.
A program may use at most 32 MiB of HBM per device.

```python
import math
import jax
import jax.numpy as jnp
from jax import lax

D = 4096
C = 4096
SHORT = 7
MEDIUM = 128
TOKENS = 24576


def level_of(key, shape, split, smallest, largest):
    factor_of, own = 1.0, jax.random.fold_in(key, 6)
    for dim, shards_of in split:
        steps = jnp.exp(jax.random.uniform(jax.random.fold_in(own, dim), (shards_of,), jnp.float32, smallest / len(split), largest / len(split)))
        factor_of = factor_of * jnp.repeat(steps, shape[dim] // shards_of).reshape([-1 if axis == dim else 1 for axis in range(len(shape))])
    return factor_of


def gaussian(key, extent, width, limit, shards=(), kind=jnp.bfloat16):
    array = width * jax.random.normal(key, extent, jnp.float32)
    if shards:
        array = array * level_of(key, extent, shards, -0.22, 0.18)
    return jnp.clip(array, -limit, limit).astype(kind)


def setup_inputs(seed: int = 0) -> dict:
    splits = jax.random.split(jax.random.key(seed), 8)
    return {
        "query_feat": gaussian(splits[0], (TOKENS, C), 1.0, 6.0, ((0, 128), (1, 8)), jnp.float32),
        "key_feat": gaussian(splits[1], (TOKENS, C), 1.0, 6.0, ((0, 128), (1, 8)), jnp.float32),
        "value_feat": gaussian(splits[2], (TOKENS, C), 1.0, 6.0, ((0, 128), (1, 8)), jnp.float32),
        "short_filter": gaussian(splits[3], (3, SHORT, C), 0.4, 3.0, ((2, 8),), jnp.float32),
        "medium_filter": gaussian(splits[4], (MEDIUM, C), 0.1, 0.6, ((1, 8),), jnp.float32),
        "out_weight": gaussian(splits[5], (C, D), C ** -0.5, 0.09375, ((0, 8),)),
        "cotangent": gaussian(splits[6], (TOKENS, D), 1.0, 6.0, ((0, 128), (1, 8))),
    }


def causal_conv(extended, filter_taps):
    taps = filter_taps.shape[0]
    count = extended.shape[0] - taps + 1

    def add_tap(index, total):
        start = (taps - 1 - index).astype(jnp.int32)
        return total + filter_taps[index] * lax.dynamic_slice_in_dim(extended, start, count, 0)
    return lax.fori_loop(jnp.int32(0), jnp.int32(taps), add_tap, jnp.zeros((count, extended.shape[1]), extended.dtype))

def reverse_conv(extended, filter_taps):
    taps = filter_taps.shape[0]
    count = extended.shape[0] - taps + 1

    def add_tap(index, total):
        start = index.astype(jnp.int32)
        return total + filter_taps[index] * lax.dynamic_slice_in_dim(extended, start, count, 0)
    return lax.fori_loop(jnp.int32(0), jnp.int32(taps), add_tap, jnp.zeros((count, extended.shape[1]), extended.dtype))

def taps_grad(extended, grad_rows):
    count = grad_rows.shape[0]
    taps = extended.shape[0] - count + 1

    def one_tap(index):
        start = (taps - 1 - index).astype(jnp.int32)
        return lax.optimization_barrier(jnp.sum(grad_rows * lax.dynamic_slice_in_dim(extended, start, count, 0), axis=0))
    return lax.map(one_tap, jnp.arange(taps, dtype=jnp.int32))

def reference(query_feat, key_feat, value_feat, short_filter, medium_filter, out_weight, cotangent):
    short_len = short_filter.shape[1]
    medium_len = medium_filter.shape[0]
    front_short = ((short_len - 1, 0), (0, 0))
    back_short = ((0, short_len - 1), (0, 0))
    query_ext = jnp.pad(query_feat, front_short)
    key_ext = jnp.pad(key_feat, front_short)
    value_ext = jnp.pad(value_feat, front_short)
    query_short = causal_conv(query_ext, short_filter[0])
    key_short = causal_conv(key_ext, short_filter[1])
    value_short = causal_conv(value_ext, short_filter[2])
    gated = key_short * value_short
    gated_ext = jnp.pad(gated, ((medium_len - 1, 0), (0, 0)))
    mixed = causal_conv(gated_ext, medium_filter)
    gated_out = (query_short * mixed).astype(jnp.bfloat16)
    block_out = jnp.dot(gated_out, out_weight, preferred_element_type=jnp.float32)
    grad_gated = jnp.dot(cotangent, out_weight.T, preferred_element_type=jnp.float32)
    grad_qshort = grad_gated * mixed
    grad_mixed = grad_gated * query_short
    grad_prod = reverse_conv(jnp.pad(grad_mixed, ((0, medium_len - 1), (0, 0))), medium_filter)
    grad_kshort = grad_prod * value_short
    grad_vshort = grad_prod * key_short
    grad_query = reverse_conv(jnp.pad(grad_qshort, back_short), short_filter[0])
    grad_key = reverse_conv(jnp.pad(grad_kshort, back_short), short_filter[1])
    grad_value = reverse_conv(jnp.pad(grad_vshort, back_short), short_filter[2])
    norm_scale = 1.0 / math.sqrt(TOKENS)
    grad_medium = taps_grad(gated_ext, grad_mixed) * norm_scale
    grad_short = jnp.stack([taps_grad(query_ext, grad_qshort), taps_grad(key_ext, grad_kshort), taps_grad(value_ext, grad_vshort)]) * norm_scale
    return (block_out, grad_query, grad_key, grad_value, grad_short, grad_medium)
```

```python
import functools
import math

import jax
import jax.numpy as jnp
from jax import lax
from jax.experimental import pallas as pl
from jax.experimental.pallas import tpu as pltpu
from jax.sharding import PartitionSpec as P

LANES = 128
SEQ = ("chip", "core")
PARAMS = pltpu.CompilerParams(vmem_limit_bytes=16 << 20)
EDGE = 8


def from_behind(block, axis, distance):
    devices = range(lax.axis_size(axis))
    route = [(i - distance, i) for i in devices if i - distance in devices]
    return lax.ppermute(block, axis, route)


def tile(ref, index):
    return ref[8 * index : 8 * index + 8, :]


def row_sum(value):
    return jnp.sum(value, axis=0, keepdims=True)


def short_convs(
    query_ref, key_ref, value_ref, rims_ref, taps_ref,
    qext_ref, kext_ref, vext_ref, qshort_ref, kshort_ref, vshort_ref, gated_ref, tail_ref, heads_ref,
):
    rows = query_ref.shape[0]
    arrays = ((query_ref, qext_ref, qshort_ref), (key_ref, kext_ref, kshort_ref), (value_ref, vext_ref, vshort_ref))
    for i, (feat_ref, ext_ref, out_ref) in enumerate(arrays):
        ext_ref[:EDGE, :] = rims_ref[EDGE * i : EDGE * (i + 1), :]
        ext_ref[EDGE:, :] = feat_ref[...]
        total = None
        for j in range(taps_ref.shape[1]):
            part = ext_ref[EDGE - j : EDGE - j + rows, :] * taps_ref[i, j : j + 1, :]
            total = part if total is None else total + part
        out_ref[...] = total
    gated = kshort_ref[...] * vshort_ref[...]
    gated_ref[...] = gated
    tail_ref[...] = gated[rows - tail_ref.shape[0] :]
    heads_ref[:EDGE, :] = kshort_ref[:EDGE, :]
    heads_ref[EDGE:, :] = vshort_ref[:EDGE, :]


def medium_conv(gated_ref, rim_ref, taps_ref, qshort_ref, ext_ref, mixed_ref, out_ref, shift_ref):
    rows = gated_ref.shape[0] // 8
    taps = taps_ref.shape[0]
    groups = taps // 8
    length = 8 * (rows + groups - 1)
    ext_ref[:taps, :] = rim_ref[...]
    ext_ref[taps:, :] = gated_ref[...]
    for s in range(8):
        shift_ref[s] = ext_ref[1 + s : 1 + s + length, :]
    totals = slide(shift_ref, lambda a, s: taps_ref[pl.ds(taps - 1 - 8 * a - s, 1), :], rows, groups)
    for r in range(rows):
        mixed_ref[8 * r : 8 * r + 8, :] = totals[r]
    out_ref[...] = (qshort_ref[...] * mixed_ref[...]).astype(out_ref.dtype)


def slide(shift_ref, tap_of, rows, groups):
    def step(s, totals):
        view = shift_ref.at[s]
        weights = [jnp.broadcast_to(tap_of(a, s), (8, LANES)) for a in range(groups)]
        totals = list(totals)
        for m in range(rows + groups - 1):
            block = tile(view, m)
            for a in range(max(0, m - rows + 1), min(groups, m + 1)):
                totals[m - a] = totals[m - a] + block * weights[a]
        return tuple(totals)

    return lax.fori_loop(0, 8, step, (jnp.zeros((8, LANES), jnp.float32),) * rows)


def project(gated_ref, weight_ref, out_ref):
    out_ref[...] = jnp.dot(gated_ref[...], weight_ref[...], preferred_element_type=jnp.float32)


def gate_grads(cot_ref, weight_ref, mixed_ref, query_ref, qgrad_ref, mgrad_ref, rim_ref):
    parts, _, width = cot_ref.shape
    total = None
    for i in range(parts):
        part = lax.dot_general(
            cot_ref[i],
            weight_ref[:, width * i : width * (i + 1)],
            (((1,), (1,)), ((), ())),
            preferred_element_type=jnp.float32,
        )
        total = part if total is None else total + part
    qgrad = total * mixed_ref[...]
    mgrad = total * query_ref[...]
    qgrad_ref[...] = qgrad
    mgrad_ref[...] = mgrad
    rim = jnp.concatenate([mgrad[: rim_ref.shape[0] - EDGE], qgrad[:EDGE]], axis=0)
    rim_ref[...] = rim.astype(rim_ref.dtype)


def short_rows(grad_ref, ext_ref, out_ref, taps):
    rows = ext_ref.shape[0] - EDGE
    out_ref[...] = jnp.zeros(out_ref.shape, jnp.float32)
    for j in range(taps):
        out_ref[j : j + 1, :] = row_sum(grad_ref[:rows, :] * ext_ref[EDGE - j : EDGE - j + rows, :])


def medium_terms(mgrad_ref, ext_ref, qgrad_ref, qext_ref, terms_ref, qterms_ref, shift_ref, acc_ref, *, taps, short):
    rows = mgrad_ref.shape[0] // 8
    groups = taps // 8
    length = 8 * (rows + groups - 1)
    for s in range(8):
        shift_ref[s] = ext_ref[1 + s : 1 + s + length, :]

    grads = [tile(mgrad_ref, r) for r in range(rows)]

    def step(s, carry):
        view = shift_ref.at[s]
        accs = [None] * groups
        for m in range(rows + groups - 1):
            block = tile(view, m)
            for a in range(max(0, m - rows + 1), min(groups, m + 1)):
                part = block * grads[m - a]
                accs[a] = part if accs[a] is None else accs[a] + part
        for a in range(groups):
            acc_ref[s, 8 * a : 8 * a + 8, :] = accs[a]
        return carry

    lax.fori_loop(0, 8, step, 0)
    for s in range(8):
        for a in range(groups):
            j = taps - 1 - (8 * a + s)
            terms_ref[j : j + 1, :] = row_sum(acc_ref[s, 8 * a : 8 * a + 8, :])
    short_rows(qgrad_ref, qext_ref, qterms_ref, short)


def product_grads(
    mgrad_ref, rim_ref, taps_ref, key_ref, value_ref, heads_ref, kext_ref, vext_ref, terms_ref, qterms_ref,
    kgrad_ref, vgrad_ref, packed_ref, ext_ref, shift_ref, prod_ref, small_ref, *, short,
):
    own = mgrad_ref.shape[0]
    rows = prod_ref.shape[0] // 8
    groups = taps_ref.shape[0] // 8
    length = shift_ref.shape[1]
    ext_ref[:own, :] = mgrad_ref[...]
    ext_ref[own:, :] = rim_ref[...].astype(jnp.float32)[: ext_ref.shape[0] - own]
    for s in range(8):
        shift_ref[s] = ext_ref[s : s + length, :]
    totals = slide(shift_ref, lambda a, s: taps_ref[pl.ds(8 * a + s, 1), :], rows, groups)
    zero = jnp.zeros((8, LANES), jnp.float32)
    for r in range(rows):
        prod_ref[8 * r : 8 * r + 8, :] = totals[r]
    kgrad_ref[:own, :] = prod_ref[:own, :] * value_ref[...]
    vgrad_ref[:own, :] = prod_ref[:own, :] * key_ref[...]
    kgrad_ref[own:, :] = prod_ref[own:, :] * heads_ref[EDGE:, :]
    vgrad_ref[own:, :] = prod_ref[own:, :] * heads_ref[:EDGE, :]
    short_rows(kgrad_ref, kext_ref, small_ref.at[0], short)
    short_rows(vgrad_ref, vext_ref, small_ref.at[1], short)
    tiles = [tile(terms_ref, i) for i in range(groups)] + [qterms_ref[...], small_ref[0], small_ref[1]]
    across = packed_ref.shape[2] // LANES
    for place in range(packed_ref.shape[0] // 8 * across):
        k, q = divmod(place, across)
        packed_ref[8 * k : 8 * k + 8, 0, LANES * q : LANES * (q + 1)] = tiles[place] if place < len(tiles) else zero


def unpack(packed_ref, medium_ref, short_ref):
    across = packed_ref.shape[2] // LANES
    groups = medium_ref.shape[0] // 8

    def at(place):
        k, q = divmod(place, across)
        return packed_ref[8 * k : 8 * k + 8, 0, LANES * q : LANES * (q + 1)]

    for i in range(groups):
        medium_ref[8 * i : 8 * i + 8, :] = at(i)
    for i in range(short_ref.shape[0]):
        short_ref[i] = at(groups + i)[: short_ref.shape[1]]


def feature_grads(qgrad_ref, rim_ref, kgrad_ref, vgrad_ref, taps_ref, gq_ref, gk_ref, gv_ref, ext_ref):
    rows = qgrad_ref.shape[0]
    ext_ref[:rows, :] = qgrad_ref[...]
    ext_ref[rows:, :] = rim_ref[...].astype(jnp.float32)[rim_ref.shape[0] - EDGE :]
    for i, (grad_ref, out_ref) in enumerate(((ext_ref, gq_ref), (kgrad_ref, gk_ref), (vgrad_ref, gv_ref))):
        total = None
        for j in range(taps_ref.shape[1]):
            part = grad_ref[j : j + rows, :] * taps_ref[i, j : j + 1, :]
            total = part if total is None else total + part
        out_ref[...] = total


def in_hbm(array):
    return pltpu.with_memory_space_constraint(array, pltpu.HBM)


def lanes(rows, width=LANES):
    return pl.BlockSpec((rows, width), lambda b: (0, b))


def f32(*shape):
    return jax.ShapeDtypeStruct(shape, jnp.float32)


def shards(query_feat, key_feat, value_feat, short_filter, medium_filter, out_weight, cotangent):
    rows, channels = query_feat.shape
    short = short_filter.shape[1]
    taps = medium_filter.shape[0]
    devices = lax.axis_size(SEQ)
    blocks = channels // LANES
    grid = (blocks,)

    tiles = lax.axis_size("tile")
    with jax.named_scope("cot_exchange"):
        cot_parts = lax.all_to_all(jnp.broadcast_to(cotangent, (tiles, *cotangent.shape)), "tile", 0, 0, tiled=True)
    rims = from_behind(
        jnp.concatenate([query_feat[-EDGE:], key_feat[-EDGE:], value_feat[-EDGE:]], axis=0), SEQ, 1
    )
    query_ext, key_ext, value_ext, query_short, key_short, value_short, gated, gated_tail, heads = pl.pallas_call(
        short_convs,
        grid=grid,
        in_specs=[lanes(rows)] * 3 + [lanes(3 * EDGE), pl.BlockSpec((3, short, LANES), lambda b: (0, 0, b))],
        out_specs=[lanes(rows + EDGE)] * 3 + [lanes(rows)] * 4 + [lanes(taps), lanes(2 * EDGE)],
        out_shape=[f32(rows + EDGE, channels)] * 3 + [f32(rows, channels)] * 4 + [f32(taps, channels), f32(2 * EDGE, channels)],
        compiler_params=PARAMS,
        name="short_convs",
    )(query_feat, key_feat, value_feat, rims, short_filter)
    gated_rim = from_behind(gated_tail, SEQ, 1)
    next_heads = from_behind(heads, SEQ, -1)
    length = rows + taps - 8
    gated_ext, mixed, gated_out = pl.pallas_call(
        medium_conv,
        grid=grid,
        in_specs=[lanes(rows), lanes(taps), lanes(taps), lanes(rows)],
        out_specs=[lanes(rows + taps), lanes(rows), lanes(rows)],
        out_shape=[f32(rows + taps, channels), f32(rows, channels), jax.ShapeDtypeStruct((rows, channels), jnp.bfloat16)],
        scratch_shapes=[pltpu.VMEM((8, length, LANES), jnp.float32)],
        compiler_params=PARAMS,
        name="medium_conv",
    )(gated, gated_rim, medium_filter, query_short)
    features = out_weight.shape[1]
    column = 4 * LANES
    partial_out = pl.pallas_call(
        project,
        grid=(features // column,),
        in_specs=[
            pl.BlockSpec((rows, channels), lambda b: (0, 0)),
            pl.BlockSpec((channels, column), lambda b: (0, b)),
        ],
        out_specs=lanes(rows, column),
        out_shape=f32(rows, features),
        compiler_params=PARAMS,
        name="project",
    )(gated_out, in_hbm(out_weight))
    cot_parts, partial_out, next_heads = lax.optimization_barrier((cot_parts, partial_out, next_heads))
    block_out = lax.psum_scatter(partial_out, "tile", scatter_dimension=1, tiled=True)

    wide = 2 * LANES
    grad_qshort, grad_mixed, mixed_head = pl.pallas_call(
        gate_grads,
        grid=(channels // wide,),
        in_specs=[
            pl.BlockSpec(cot_parts.shape, lambda b: (0, 0, 0)),
            pl.BlockSpec((wide, out_weight.shape[1]), lambda b: (b, 0)),
            lanes(rows, wide),
            lanes(rows, wide),
        ],
        out_specs=[lanes(rows, wide), lanes(rows, wide), lanes(taps + 2 * EDGE, wide)],
        out_shape=[f32(rows, channels), f32(rows, channels), jax.ShapeDtypeStruct((taps + 2 * EDGE, channels), jnp.bfloat16)],
        compiler_params=PARAMS,
        name="gate_grads",
    )(in_hbm(cot_parts), in_hbm(out_weight), mixed, query_short)
    mixed_rim = from_behind(mixed_head, SEQ, -1)

    terms, query_terms = pl.pallas_call(
        functools.partial(medium_terms, taps=taps, short=short),
        grid=grid,
        in_specs=[lanes(rows), lanes(rows + taps), lanes(rows), lanes(rows + EDGE)],
        out_specs=[lanes(taps), lanes(8)],
        out_shape=[f32(taps, channels), f32(8, channels)],
        scratch_shapes=[pltpu.VMEM((8, length, LANES), jnp.float32), pltpu.VMEM((8, taps, LANES), jnp.float32)],
        compiler_params=PARAMS,
        name="medium_terms",
    )(grad_mixed, gated_ext, grad_qshort, query_ext)

    packed_rows = devices // blocks
    across = -(-(taps // 8 + 3) // (packed_rows // 8))
    packed_spec = pl.BlockSpec((packed_rows, 1, LANES * across), lambda b: (b, 0, 0))
    grad_kshort, grad_vshort, packed = pl.pallas_call(
        functools.partial(product_grads, short=short),
        grid=grid,
        in_specs=[
            lanes(rows), lanes(taps + 2 * EDGE), lanes(taps), lanes(rows), lanes(rows), lanes(2 * EDGE),
            lanes(rows + EDGE), lanes(rows + EDGE), lanes(taps), lanes(8),
        ],
        out_specs=[lanes(rows + EDGE), lanes(rows + EDGE), packed_spec],
        out_shape=[
            f32(rows + EDGE, channels),
            f32(rows + EDGE, channels),
            f32(devices, 1, LANES * across),
        ],
        scratch_shapes=[
            pltpu.VMEM((rows + taps + EDGE, LANES), jnp.float32),
            pltpu.VMEM((8, length + EDGE, LANES), jnp.float32),
            pltpu.VMEM((rows + EDGE, LANES), jnp.float32),
            pltpu.VMEM((2, 8, LANES), jnp.float32),
        ],
        compiler_params=PARAMS,
        name="product_grads",
    )(
        grad_mixed, mixed_rim, medium_filter, key_short, value_short, next_heads,
        key_ext, value_ext, terms, query_terms,
    )

    norm_scale = 1.0 / math.sqrt(devices * rows)
    chips = lax.axis_size("chip")
    pair = lax.all_to_all(packed, "core", 0, 0, tiled=True)
    halves = pair[:chips] + pair[chips:]
    parts = lax.all_to_all(halves, "chip", 0, 0, tiled=True)
    chunk = jnp.broadcast_to(jnp.sum(parts, axis=0, keepdims=True) * norm_scale, parts.shape)
    half = lax.all_to_all(chunk, "chip", 0, 0, tiled=True)
    totals = lax.all_gather(half, "core", axis=0, tiled=True)
    grad_medium, grad_short = pl.pallas_call(
        unpack,
        grid=grid,
        in_specs=[packed_spec],
        out_specs=[lanes(taps), pl.BlockSpec((3, short, LANES), lambda b: (0, 0, b))],
        out_shape=[f32(taps, channels), f32(3, short, channels)],
        compiler_params=PARAMS,
        name="unpack",
    )(totals)

    grad_query, grad_key, grad_value = pl.pallas_call(
        feature_grads,
        grid=grid,
        in_specs=[
            lanes(rows), lanes(taps + 2 * EDGE), lanes(rows + EDGE), lanes(rows + EDGE),
            pl.BlockSpec((3, short, LANES), lambda b: (0, 0, b)),
        ],
        out_specs=[lanes(rows)] * 3,
        out_shape=[f32(rows, channels)] * 3,
        scratch_shapes=[pltpu.VMEM((rows + EDGE, LANES), jnp.float32)],
        compiler_params=PARAMS,
        name="feature_grads",
    )(grad_qshort, mixed_rim, grad_kshort, grad_vshort, short_filter)
    return block_out, grad_query, grad_key, grad_value, grad_short, grad_medium


def solution(mesh):
    devices = mesh.devices
    split = jax.sharding.Mesh(devices.reshape(devices.shape[0] // 2, 2, devices.shape[1]), (*SEQ, "tile"))
    rows = P(SEQ, "tile")
    in_specs = (rows, rows, rows, P(None, None, "tile"), P(None, "tile"), P("tile", None), rows)
    out_specs = (rows, rows, rows, rows, P(None, None, "tile"), P(None, "tile"))
    return jax.shard_map(shards, mesh=split, in_specs=in_specs, out_specs=out_specs, check_vma=False)
```
